1024 devices in a mesh: band: 32 (over y, x_hi), grid: 32 (over z, x_lo, core).
Axes of the slice: x: 8 (x_hi: 4, x_lo: 2; x = x_hi * 2 + x_lo), y: 8, z: 8, core: 2. Of those that a mesh axis runs over, the one named last changes fastest.
Arguments:
- orbitals: float32 [5120, 49152], P('band', 'grid'), may hold values from -6 to 6
Outputs:
- corrected: float32 [5120, 49152], P('band', 'grid')
The draws below stay inside these ranges and needn't reach their ends.
All inputs are finite; a program needn't handle non-finite values.
Results may differ from the reference program's by a relative error of at most 0.0001.
Values sent between devices are 32-bit elements; how exact they have to be, the bound alone decides.
No kernel may reach another device: no remote copies, remote signals or barrier semaphores. Data moves between devices by JAX's collectives and lax.ppermute only.
A program may use at most 32 MiB of HBM per device.

```python
import jax
import jax.numpy as jnp
from jax import lax

BD = 160
NB = 5120
NG = 49152
SHIFTS = 4
N_BAND = 32


def shard_levels(stream_key, shape, pieces, low, high):
    loudness, own = 1.0, jax.random.fold_in(stream_key, 6)
    for dim, blocks in pieces:
        steps = jnp.exp(jax.random.uniform(jax.random.fold_in(own, dim), (blocks,), jnp.float32, low / len(pieces), high / len(pieces)))
        loudness = loudness * jnp.repeat(steps, shape[dim] // blocks).reshape([-1 if axis == dim else 1 for axis in range(len(shape))])
    return loudness


def noise(key, extent, deviation, reach, split=(), kind=jnp.bfloat16):
    entries = jax.random.normal(key, extent, jnp.float32) * deviation
    if len(split) > 0:
        entries = shard_levels(key, extent, split, -0.22, 0.18) * entries
    return jnp.clip(entries, min=-reach, max=reach).astype(kind)


def setup_inputs(seed: int = 0) -> dict:
    splits = jax.random.split(jax.random.key(seed), 2)
    orbitals = noise(splits[0], (NB, NG), 1.0, 6.0, ((0, 32), (1, 32)), jnp.float32)
    return dict(orbitals=orbitals)


def reference(orbitals):
    highest = lax.Precision.HIGHEST
    blocks = orbitals.reshape(N_BAND, BD, NG)
    identity = jnp.eye(BD, dtype=jnp.float32)

    def correlation(left, right):
        return jnp.einsum("bin,bjn->bij", left, right, precision=highest) / NG

    tile = correlation(blocks, blocks)
    fix = jnp.einsum("bij,bjn->bin", tile - identity, blocks, precision=highest)
    for shift_count in range(1, SHIFTS + 1):
        other = jnp.roll(blocks, shift_count, axis=0)
        tile = correlation(blocks, other)
        fix = fix + jnp.einsum("bij,bjn->bin", tile, other, precision=highest)
        backward = jnp.einsum("bji,bjn->bin", tile, blocks, precision=highest)
        fix = fix + jnp.roll(backward, -shift_count, axis=0)
    return orbitals - 0.5 * fix.reshape(N_BAND * BD, NG)
```

```python
import jax
import jax.numpy as jnp
from jax import lax
from jax.sharding import Mesh, PartitionSpec as P

RING = ("xh", "z", "xl")
ROWS, UNIT = 8, 128


def passed_along(block, distance):
    count = lax.axis_size("y")
    return lax.ppermute(block, "y", [(i, (i + distance) % count) for i in range(count)])


def exchange(pieces, axes):
    return lax.all_to_all(pieces, axes, 0, 0)


def spread(piece, axes):
    count = lax.axis_size(axes)
    return exchange(jnp.broadcast_to(piece[None], (count, *piece.shape)), axes)


def product(left, right, dims, precision=lax.Precision.HIGHEST):
    return lax.dot_general(left, right, (dims, ((), ())), precision=precision, preferred_element_type=jnp.float32)


def packed(wide, middle, narrow, single):
    bands = wide.shape[0]
    main = jnp.concatenate(
        [wide, middle[:, :384], narrow[:, :256], single[:, :128], middle[:, 384:], single[:, 128:]], 1
    )
    main = main.reshape(bands // ROWS, ROWS, 12, UNIT).transpose(0, 2, 1, 3).reshape(-1, ROWS, UNIT)
    half = bands // 2
    tail = jnp.concatenate([narrow[:half, 256:], narrow[half:, 256:]], 1).reshape(-1, ROWS, UNIT)
    return jnp.concatenate([main, tail, jnp.zeros((6, ROWS, UNIT), jnp.float32)])


def unpacked(units, bands):
    count = bands // ROWS * 12
    main = units[:count].reshape(bands // ROWS, 12, ROWS, UNIT).transpose(0, 2, 1, 3).reshape(bands, -1)
    tail = units[count : count + 10].reshape(bands // 2, UNIT)
    narrow_end = jnp.concatenate([tail[:, :64], tail[:, 64:]])
    wide = main[:, :640]
    middle = jnp.concatenate([main[:, 640:1024], main[:, 1408:1504]], 1)
    narrow = jnp.concatenate([main[:, 1024:1280], narrow_end], 1)
    single = jnp.concatenate([main[:, 1280:1408], main[:, 1504:]], 1)
    return wide, middle, narrow, single


def scattered(units):
    units = units.reshape(2, -1, ROWS, UNIT)
    units = exchange(units, "c").sum(0)
    units = units.reshape(lax.axis_size(RING), -1, ROWS, UNIT)
    return exchange(units, RING).sum(0)


def shards(orbitals):
    bands = orbitals.shape[0]
    parts = lax.axis_size("xh")
    points = orbitals.shape[1] * lax.axis_size(("z", "xl", "c"))
    row = exchange(orbitals.reshape(bands, parts, -1).transpose(1, 0, 2), "xh")
    below = passed_along(row, 1)
    above = passed_along(row, -1)
    along = ((1,), (1,))
    rows = row.reshape(parts * bands, -1)

    inner = [product(row[a], rows[: bands * (a + 1)], along) for a in range(parts)]
    inner = scattered(packed(inner[3], inner[2], inner[1], inner[0]))

    below, above, inner = lax.optimization_barrier((below, above, inner))
    belows = below.reshape(parts * bands, -1)
    outer = [product(row[a], belows[bands * a :], along) for a in range(parts)]
    outer = scattered(packed(outer[0], outer[1], outer[2], outer[3]))

    share = jnp.stack([inner, outer]) / points
    both = spread(share, RING)
    inner_half = both[:, 0].reshape(-1, ROWS, UNIT)
    outer_half = both[:, 1].reshape(-1, ROWS, UNIT)
    next_half = passed_along(outer_half, -1)
    inner, outer = (
        spread(half, "c").reshape(-1, ROWS, UNIT) for half in (inner_half, outer_half)
    )
    s3, s2, s1, s0 = unpacked(inner, bands)
    inner = [s0, s1, s2, s3]
    outer = unpacked(outer, bands)

    identity = jnp.eye(bands, dtype=jnp.float32)
    stacked = jnp.concatenate([belows, rows, above.reshape(parts * bands, -1)])
    fix = []
    for a in range(parts):
        own = jnp.concatenate([inner[a][:, : bands * a], inner[a][:, bands * a :] - identity], 1)
        left = jnp.concatenate([outer[a], own], 1)
        total = product(left, stacked[bands * a : bands * (a + 5)], ((1,), (0,)))
        if a < parts - 1:
            upper = jnp.concatenate([inner[b][:, bands * a : bands * (a + 1)] for b in range(a + 1, parts)])
            total += product(upper, rows[bands * (a + 1) :], ((0,), (0,)))
        fix.append(total)
    following = unpacked(spread(next_half, "c").reshape(-1, ROWS, UNIT), bands)
    for a in range(parts):
        upper = jnp.concatenate([following[b][:, bands * (a - b) : bands * (a - b + 1)] for b in range(a + 1)])
        fix[a] += product(upper, above.reshape(parts * bands, -1)[: bands * (a + 1)], ((0,), (0,)))
    corrected = row - 0.5 * jnp.stack(fix)
    return exchange(corrected, "xh").transpose(1, 0, 2).reshape(orbitals.shape)


def solution(mesh):
    fine = Mesh(mesh.devices.reshape(8, 4, 8, 2, 2), ("y", "xh", "z", "xl", "c"))
    spec = P(("y", "xh"), ("z", "xl", "c"))
    return jax.shard_map(shards, mesh=fine, in_specs=(spec,), out_specs=spec, check_vma=False)
```

```python
import functools

import jax
import jax.numpy as jnp
from jax import lax
from jax.experimental import pallas as pl
from jax.experimental.pallas import tpu as pltpu
from jax.sharding import Mesh, PartitionSpec as P

RING = ("xh", "z", "xl")
ROWS, UNIT = 8, 128
GROUPS = 4
UNITS = 256
NT = ((1,), (1,))
NN = ((1,), (0,))
TN = ((0,), (0,))


def passed_along(block, distance):
    count = lax.axis_size("y")
    return lax.ppermute(block, "y", [(i, (i + distance) % count) for i in range(count)])


def exchange(pieces, axes):
    return lax.all_to_all(pieces, axes, 0, 0)


def spread(piece, axes):
    count = lax.axis_size(axes)
    return exchange(jnp.broadcast_to(piece[None], (count, *piece.shape)), axes)


def halves(value):
    high = value.astype(jnp.bfloat16)
    return high, (value - high.astype(jnp.float32)).astype(jnp.bfloat16)


def product(left, right, dims):
    dot = functools.partial(
        lax.dot_general, dimension_numbers=(dims, ((), ())), preferred_element_type=jnp.float32
    )
    return dot(left[0], right[0]) + (dot(left[0], right[1]) + dot(left[1], right[0]))


def cut(pair, rows=slice(None), columns=slice(None)):
    return tuple(value[rows, columns] for value in pair)


def call(kernel, outs, *operands):
    return pl.pallas_call(
        kernel,
        out_shape=jax.ShapeDtypeStruct(outs, jnp.float32),
        compiler_params=pltpu.CompilerParams(vmem_limit_bytes=48 << 20),
    )(*operands)


def tiles_kernel(order, row_ref, other_ref, units_ref):
    bands = row_ref.shape[1]
    other = halves(other_ref[...].reshape(GROUPS * bands, -1))

    def put(index, value):
        count = value.shape[0] // ROWS
        units_ref[20 * index : 20 * index + count] = value.reshape(count, ROWS, UNIT)

    strips = []
    for a, first, last in order:
        left = halves(row_ref[a])
        strips.append(product(left, cut(other, slice(bands * first, bands * last)), NT))
    wide, middle, narrow, single = strips
    columns = [wide[:, UNIT * i : UNIT * (i + 1)] for i in range(5)]
    columns += [middle[:, UNIT * i : UNIT * (i + 1)] for i in range(3)]
    columns += [narrow[:, UNIT * i : UNIT * (i + 1)] for i in range(2)]
    columns += [single[:, :UNIT], jnp.concatenate([middle[:, 384:], single[:, UNIT:]], 1)]
    columns += [jnp.concatenate([narrow[: bands // 2, 256:], narrow[bands // 2 :, 256:]], 1)]
    for index, value in enumerate(columns):
        put(index, value)
    units_ref[250:] = jnp.zeros((6, ROWS, UNIT), jnp.float32)


def strips_of(units_ref, offset):
    half = UNITS // 2

    def get(index, count=20):
        start, stop = 20 * index, 20 * index + count
        parts = []
        for core in range(2):
            low, high = max(start, half * core) - half * core, min(stop, half * (core + 1)) - half * core
            if low < high:
                part = units_ref[core, low // 2 : high // 2, offset : offset + 2]
                parts.append(part.reshape(high - low, ROWS, UNIT))
        value = parts[0] if len(parts) == 1 else jnp.concatenate(parts)
        return value.reshape(count * ROWS, UNIT)

    mixed, tail = get(11), get(12, 10)
    wide = jnp.concatenate([get(i) for i in range(5)], 1)
    middle = jnp.concatenate([get(5), get(6), get(7), mixed[:, :96]], 1)
    narrow = jnp.concatenate([get(8), get(9), jnp.concatenate([tail[:, :64], tail[:, 64:]])], 1)
    single = jnp.concatenate([get(10), mixed[:, 96:]], 1)
    return wide, middle, narrow, single


def apply_kernel(row_ref, below_ref, units_ref, out_ref):
    bands = row_ref.shape[1]
    rows = halves(row_ref[...].reshape(GROUPS * bands, -1))
    below = halves(below_ref[...].reshape(GROUPS * bands, -1))
    inner = strips_of(units_ref, 0)[::-1]
    outer = strips_of(units_ref, 2)
    fix = []
    for a in range(GROUPS):
        width = bands * (a + 1)
        shift = lax.broadcasted_iota(jnp.int32, (bands, width), 1) - lax.broadcasted_iota(
            jnp.int32, (bands, width), 0
        )
        own = halves(jnp.where(shift == bands * a, inner[a] - 1.0, inner[a]))
        total = product(own, cut(rows, slice(0, width)), NN)
        total += product(halves(outer[a]), cut(below, slice(bands * a, None)), NN)
        fix.append(total)
        if a > 0:
            back = product(
                cut(own, slice(None), slice(0, bands * a)), cut(rows, slice(bands * a, width)), TN
            )
            for b in range(a):
                fix[b] += back[bands * b : bands * (b + 1)]
    for a in range(GROUPS):
        out_ref[a] = row_ref[a] - 0.5 * fix[a]


def above_kernel(part_ref, above_ref, units_ref, out_ref):
    bands = part_ref.shape[1]
    above = halves(above_ref[...].reshape(GROUPS * bands, -1))
    strips = strips_of(units_ref, 0)
    fix = [None] * GROUPS
    for b in range(GROUPS):
        back = product(halves(strips[b]), cut(above, slice(bands * b, bands * (b + 1))), TN)
        for a in range(b, GROUPS):
            term = back[bands * (a - b) : bands * (a - b + 1)]
            fix[a] = term if b == 0 else fix[a] + term
    for a in range(GROUPS):
        out_ref[a] = part_ref[a] - 0.5 * fix[a]


INNER = [(3, 0, 4), (2, 0, 3), (1, 0, 2), (0, 0, 1)]
OUTER = [(0, 0, 4), (1, 1, 4), (2, 2, 4), (3, 3, 4)]


def shards(orbitals):
    bands = orbitals.shape[0]
    points = orbitals.shape[1] * lax.axis_size(("z", "xl", "c"))
    members = lax.axis_size(RING)
    row = exchange(orbitals.reshape(bands, GROUPS, -1).transpose(1, 0, 2), "xh")
    below = passed_along(row, 1)
    above = passed_along(row, -1)

    def tiles(order, other):
        units = call(functools.partial(tiles_kernel, order), (UNITS, ROWS, UNIT), row, other)
        pair = exchange(units.reshape(2, UNITS // 2, ROWS, UNIT), "c")
        return (pair[0] + pair[1]).reshape(members, -1, ROWS, UNIT)

    inner = tiles(INNER, row)
    below, above, inner = lax.optimization_barrier((below, above, inner))
    outer = tiles(OUTER, below)
    share = exchange(jnp.concatenate([inner, outer], 1), RING).sum(0) / points

    both = spread(share, RING)
    following = passed_along(both[:, 2:], -1)
    part = call(apply_kernel, row.shape, row, below, spread(both, "c"))
    corrected = call(above_kernel, row.shape, part, above, spread(following, "c"))
    return exchange(corrected, "xh").transpose(1, 0, 2).reshape(orbitals.shape)


def solution(mesh):
    fine = Mesh(mesh.devices.reshape(8, 4, 8, 2, 2), ("y", "xh", "z", "xl", "c"))
    spec = P(("y", "xh"), ("z", "xl", "c"))
    return jax.shard_map(shards, mesh=fine, in_specs=(spec,), out_specs=spec, check_vma=False)
```

```python
import functools

import jax
import jax.numpy as jnp
from jax import lax
from jax.experimental import pallas as pl
from jax.experimental.pallas import tpu as pltpu
from jax.sharding import Mesh, PartitionSpec as P


RING = ("xh", "z", "xl")
ROWS, UNIT = 8, 128
GROUPS = 4
UNITS = 256
NT = ((1,), (1,))
NN = ((1,), (0,))
TN = ((0,), (0,))


def passed_along(block, distance):
    count = lax.axis_size("y")
    return lax.ppermute(block, "y", [(i, (i + distance) % count) for i in range(count)])


def exchange(pieces, axes):
    return lax.all_to_all(pieces, axes, 0, 0)


def spread(piece, axes):
    count = lax.axis_size(axes)
    return exchange(jnp.broadcast_to(piece[None], (count, *piece.shape)), axes)


def halves(value):
    high = value.astype(jnp.bfloat16)
    return high, (value - high.astype(jnp.float32)).astype(jnp.bfloat16)


def product(left, right, dims):
    dot = functools.partial(
        lax.dot_general, dimension_numbers=(dims, ((), ())), preferred_element_type=jnp.float32
    )
    return dot(left[0], right[0]) + (dot(left[0], right[1]) + dot(left[1], right[0]))


def cut(pair, rows=slice(None), columns=slice(None)):
    return tuple(value[rows, columns] for value in pair)


def call(kernel, outs, *operands):
    return pl.pallas_call(
        kernel,
        out_shape=jax.ShapeDtypeStruct(outs, jnp.float32),
        compiler_params=pltpu.CompilerParams(vmem_limit_bytes=48 << 20),
    )(*operands)


def joined(head_ref, tail_ref):
    value = jnp.concatenate([head_ref[...], tail_ref[...]], -1)
    return value.reshape(-1, value.shape[-1])


def tiles_kernel(order, row_head, row_tail, *refs):
    *other_refs, units_ref = refs
    bands = row_head.shape[1]
    rows = halves(joined(row_head, row_tail))
    other = halves(joined(*other_refs)) if other_refs else rows

    def put(index, value):
        count = value.shape[0] // ROWS
        units_ref[20 * index : 20 * index + count] = value.reshape(count, ROWS, UNIT)

    strips = []
    for a, first, last in order:
        left = cut(rows, slice(bands * a, bands * (a + 1)))
        strips.append(product(left, cut(other, slice(bands * first, bands * last)), NT))
    wide, middle, narrow, single = strips
    columns = [wide[:, UNIT * i : UNIT * (i + 1)] for i in range(5)]
    columns += [middle[:, UNIT * i : UNIT * (i + 1)] for i in range(3)]
    columns += [narrow[:, UNIT * i : UNIT * (i + 1)] for i in range(2)]
    columns += [single[:, :UNIT], jnp.concatenate([middle[:, 384:], single[:, UNIT:]], 1)]
    columns += [jnp.concatenate([narrow[: bands // 2, 256:], narrow[bands // 2 :, 256:]], 1)]
    for index, value in enumerate(columns):
        put(index, value)
    units_ref[250:] = jnp.zeros((6, ROWS, UNIT), jnp.float32)


def strips_of(units_ref, offset):
    half = UNITS // 2

    def get(index, count=20):
        start, stop = 20 * index, 20 * index + count
        parts = []
        for core in range(2):
            low, high = max(start, half * core) - half * core, min(stop, half * (core + 1)) - half * core
            if low < high:
                part = units_ref[core, low // 2 : high // 2, offset : offset + 2]
                parts.append(part.reshape(high - low, ROWS, UNIT))
        value = parts[0] if len(parts) == 1 else jnp.concatenate(parts)
        return value.reshape(count * ROWS, UNIT)

    mixed, tail = get(11), get(12, 10)
    wide = jnp.concatenate([get(i) for i in range(5)], 1)
    middle = jnp.concatenate([get(5), get(6), get(7), mixed[:, :96]], 1)
    narrow = jnp.concatenate([get(8), get(9), jnp.concatenate([tail[:, :64], tail[:, 64:]])], 1)
    single = jnp.concatenate([get(10), mixed[:, 96:]], 1)
    return wide, middle, narrow, single


def apply_kernel(row_head, row_tail, below_head, below_tail, units_ref, out_ref):
    bands = row_head.shape[1]
    row = joined(row_head, row_tail)
    rows = halves(row)
    below = halves(joined(below_head, below_tail))
    inner = strips_of(units_ref, 0)[::-1]
    outer = strips_of(units_ref, 2)
    fix = []
    for a in range(GROUPS):
        width = bands * (a + 1)
        shift = lax.broadcasted_iota(jnp.int32, (bands, width), 1) - lax.broadcasted_iota(
            jnp.int32, (bands, width), 0
        )
        own = halves(jnp.where(shift == bands * a, inner[a] - 1.0, inner[a]))
        total = product(own, cut(rows, slice(0, width)), NN)
        total += product(halves(outer[a]), cut(below, slice(bands * a, None)), NN)
        fix.append(total)
        if a > 0:
            back = product(
                cut(own, slice(None), slice(0, bands * a)), cut(rows, slice(bands * a, width)), TN
            )
            for b in range(a):
                fix[b] += back[bands * b : bands * (b + 1)]
    for a in range(GROUPS):
        out_ref[a] = row[bands * a : bands * (a + 1)] - 0.5 * fix[a]


def above_kernel(part_ref, above_head, above_tail, units_ref, out_ref):
    bands = part_ref.shape[1]
    above = halves(joined(above_head, above_tail))
    strips = strips_of(units_ref, 0)
    fix = [None] * GROUPS
    for b in range(GROUPS):
        back = product(halves(strips[b]), cut(above, slice(bands * b, bands * (b + 1))), TN)
        for a in range(b, GROUPS):
            term = back[bands * (a - b) : bands * (a - b + 1)]
            fix[a] = term if b == 0 else fix[a] + term
    for a in range(GROUPS):
        out_ref[a] = part_ref[a] - 0.5 * fix[a]


INNER = [(3, 0, 4), (2, 0, 3), (1, 0, 2), (0, 0, 1)]
OUTER = [(0, 0, 4), (1, 1, 4), (2, 2, 4), (3, 3, 4)]


def shards(orbitals):
    bands = orbitals.shape[0]
    points = orbitals.shape[1] * lax.axis_size(("z", "xl", "c"))
    members = lax.axis_size(RING)
    width = orbitals.shape[1] // GROUPS
    split = width // 3 * 2
    pieces = [orbitals[:, width * a : width * (a + 1)] for a in range(GROUPS)]
    head = exchange(jnp.stack([piece[:, :split] for piece in pieces]), "xh")
    below_head = passed_along(head, 1)
    tail = exchange(jnp.stack([piece[:, split:] for piece in pieces]), "xh")
    below_tail = passed_along(tail, 1)
    above_head = passed_along(head, -1)
    above_tail = passed_along(tail, -1)

    def tiles(order, *operands):
        units = call(functools.partial(tiles_kernel, order), (UNITS, ROWS, UNIT), *operands)
        pair = exchange(units.reshape(2, UNITS // 2, ROWS, UNIT), "c")
        return (pair[0] + pair[1]).reshape(members, -1, ROWS, UNIT)

    inner = tiles(INNER, head, tail)
    below_head, below_tail, inner = lax.optimization_barrier((below_head, below_tail, inner))
    outer = tiles(OUTER, head, tail, below_head, below_tail)
    share = exchange(jnp.concatenate([inner, outer], 1), RING)
    share = share.sum(0) / points
    both = spread(share, RING)
    following = passed_along(both[:, 2:], -1)
    shape = (GROUPS, bands, width)
    part = call(apply_kernel, shape, head, tail, below_head, below_tail, spread(both, "c"))
    corrected = call(above_kernel, shape, part, above_head, above_tail, spread(following, "c"))
    return exchange(corrected, "xh").transpose(1, 0, 2).reshape(orbitals.shape)


def solution(mesh):
    fine = Mesh(mesh.devices.reshape(8, 4, 8, 2, 2), ("y", "xh", "z", "xl", "c"))
    spec = P(("y", "xh"), ("z", "xl", "c"))
    return jax.shard_map(shards, mesh=fine, in_specs=(spec,), out_specs=spec, check_vma=False)
```

```python
import functools

import jax
import jax.numpy as jnp
from jax import lax
from jax.experimental import pallas as pl
from jax.experimental.pallas import tpu as pltpu
from jax.sharding import Mesh, PartitionSpec as P


RING = ("xh", "z", "xl")
ROWS, UNIT = 8, 128
GROUPS = 4
UNITS = 256
NT = ((1,), (1,))
NN = ((1,), (0,))
TN = ((0,), (0,))


def passed_along(block, distance):
    count = lax.axis_size("y")
    return lax.ppermute(block, "y", [(i, (i + distance) % count) for i in range(count)])


def exchange(pieces, axes):
    return lax.all_to_all(pieces, axes, 0, 0)


def spread(piece, axes):
    count = lax.axis_size(axes)
    return exchange(jnp.broadcast_to(piece[None], (count, *piece.shape)), axes)


def halves(value):
    high = value.astype(jnp.bfloat16)
    return high, (value - high.astype(jnp.float32)).astype(jnp.bfloat16)


def product(left, right, dims):
    dot = functools.partial(
        lax.dot_general, dimension_numbers=(dims, ((), ())), preferred_element_type=jnp.float32
    )
    return dot(left[0], right[0]) + (dot(left[0], right[1]) + dot(left[1], right[0]))


def cut(pair, rows=slice(None), columns=slice(None)):
    return tuple(value[rows, columns] for value in pair)


def call(kernel, outs, *operands):
    return pl.pallas_call(
        kernel,
        out_shape=jax.ShapeDtypeStruct(outs, jnp.float32),
        compiler_params=pltpu.CompilerParams(vmem_limit_bytes=16 << 20),
    )(*operands)


def moved(copies, sems):
    copies = [pltpu.make_async_copy(*copy, sems.at[i]) for i, copy in enumerate(copies)]
    for copy in copies:
        copy.start()
    for copy in copies:
        copy.wait()


def deal_kernel(block, head, tail, sems):
    split, width = head.shape[2], head.shape[2] + tail.shape[2]
    copies = [(block.at[:, width * a : width * a + split], head.at[a]) for a in range(GROUPS)]
    copies += [(block.at[:, width * a + split : width * (a + 1)], tail.at[a]) for a in range(GROUPS)]
    moved(copies, sems)


def deal(block):
    bands, width = block.shape[0], block.shape[1] // GROUPS
    split = width // 3 * 2
    return pl.pallas_call(
        deal_kernel,
        out_shape=[
            jax.ShapeDtypeStruct((GROUPS, bands, size), jnp.float32) for size in (split, width - split)
        ],
        in_specs=[pl.BlockSpec(memory_space=pltpu.HBM)],
        out_specs=[pl.BlockSpec(memory_space=pltpu.VMEM)] * 2,
        scratch_shapes=[pltpu.SemaphoreType.DMA((2 * GROUPS,))],
        compiler_params=pltpu.CompilerParams(vmem_limit_bytes=4 << 20),
    )(block)


def collect_kernel(quarters, block, sems):
    width = quarters.shape[2]
    moved([(quarters.at[a], block.at[:, width * a : width * (a + 1)]) for a in range(GROUPS)], sems)


def collect(quarters):
    return pl.pallas_call(
        collect_kernel,
        out_shape=jax.ShapeDtypeStruct((quarters.shape[1], GROUPS * quarters.shape[2]), jnp.float32),
        in_specs=[pl.BlockSpec(memory_space=pltpu.VMEM)],
        out_specs=pl.BlockSpec(memory_space=pltpu.HBM),
        scratch_shapes=[pltpu.SemaphoreType.DMA((GROUPS,))],
        compiler_params=pltpu.CompilerParams(vmem_limit_bytes=4 << 20),
    )(quarters)


def joined(head_ref, tail_ref):
    value = jnp.concatenate([head_ref[...], tail_ref[...]], -1)
    return value.reshape(-1, value.shape[-1])


def tiles_kernel(order, row_head, row_tail, *refs):
    *other_refs, units_ref = refs
    bands = row_head.shape[1]
    rows = halves(joined(row_head, row_tail))
    other = halves(joined(*other_refs)) if other_refs else rows

    def put(index, value):
        count = value.shape[0] // ROWS
        units_ref[20 * index : 20 * index + count] = value.reshape(count, ROWS, UNIT)

    strips = []
    for a, first, last in order:
        left = cut(rows, slice(bands * a, bands * (a + 1)))
        strips.append(product(left, cut(other, slice(bands * first, bands * last)), NT))
    wide, middle, narrow, single = strips
    columns = [wide[:, UNIT * i : UNIT * (i + 1)] for i in range(5)]
    columns += [middle[:, UNIT * i : UNIT * (i + 1)] for i in range(3)]
    columns += [narrow[:, UNIT * i : UNIT * (i + 1)] for i in range(2)]
    columns += [single[:, :UNIT], jnp.concatenate([middle[:, 384:], single[:, UNIT:]], 1)]
    columns += [jnp.concatenate([narrow[: bands // 2, 256:], narrow[bands // 2 :, 256:]], 1)]
    for index, value in enumerate(columns):
        put(index, value)
    units_ref[250:] = jnp.zeros((6, ROWS, UNIT), jnp.float32)


def strips_of(units_of):
    half = UNITS // 2

    def get(index, count=20):
        start, stop = 20 * index, 20 * index + count
        parts = []
        for core in range(2):
            low, high = max(start, half * core) - half * core, min(stop, half * (core + 1)) - half * core
            if low < high:
                part = units_of(core, slice(low // 2, high // 2))
                parts.append(part.reshape(high - low, ROWS, UNIT))
        value = parts[0] if len(parts) == 1 else jnp.concatenate(parts)
        return value.reshape(count * ROWS, UNIT)

    mixed, tail = get(11), get(12, 10)
    wide = jnp.concatenate([get(i) for i in range(5)], 1)
    middle = jnp.concatenate([get(5), get(6), get(7), mixed[:, :96]], 1)
    narrow = jnp.concatenate([get(8), get(9), jnp.concatenate([tail[:, :64], tail[:, 64:]])], 1)
    single = jnp.concatenate([get(10), mixed[:, 96:]], 1)
    return wide, middle, narrow, single


def apply_kernel(row_head, row_tail, below_head, below_tail, units_ref, out_ref):
    bands = row_head.shape[1]
    row = joined(row_head, row_tail)
    rows = halves(row)
    below = halves(joined(below_head, below_tail))
    inner = strips_of(lambda core, pairs: units_ref[core, pairs, 0:2])[::-1]
    outer = strips_of(lambda core, pairs: units_ref[core, pairs, 2:4])
    fix = []
    for a in range(GROUPS):
        width = bands * (a + 1)
        shift = lax.broadcasted_iota(jnp.int32, (bands, width), 1) - lax.broadcasted_iota(
            jnp.int32, (bands, width), 0
        )
        own = halves(jnp.where(shift == bands * a, inner[a] - 1.0, inner[a]))
        total = product(own, cut(rows, slice(0, width)), NN)
        total += product(halves(outer[a]), cut(below, slice(bands * a, None)), NN)
        fix.append(total)
        if a > 0:
            back = product(
                cut(own, slice(None), slice(0, bands * a)), cut(rows, slice(bands * a, width)), TN
            )
            for b in range(a):
                fix[b] += back[bands * b : bands * (b + 1)]
    for a in range(GROUPS):
        out_ref[a] = row[bands * a : bands * (a + 1)] - 0.5 * fix[a]


def above_kernel(core_ref, part_ref, above_head, above_tail, own_ref, partner_ref, out_ref):
    first = core_ref[0] == 0
    bands = part_ref.shape[1]
    above = halves(joined(above_head, above_tail))

    def units_of(core, pairs):
        own, partner = own_ref[pairs], partner_ref[pairs]
        return jnp.where(first, own, partner) if core == 0 else jnp.where(first, partner, own)

    strips = strips_of(units_of)
    fix = [None] * GROUPS
    for b in range(GROUPS):
        back = product(halves(strips[b]), cut(above, slice(bands * b, bands * (b + 1))), TN)
        for a in range(b, GROUPS):
            term = back[bands * (a - b) : bands * (a - b + 1)]
            fix[a] = term if b == 0 else fix[a] + term
    for a in range(GROUPS):
        out_ref[a] = part_ref[a] - 0.5 * fix[a]


INNER = [(3, 0, 4), (2, 0, 3), (1, 0, 2), (0, 0, 1)]
OUTER = [(0, 0, 4), (1, 1, 4), (2, 2, 4), (3, 3, 4)]


def shards(orbitals):
    bands = orbitals.shape[0]
    points = orbitals.shape[1] * lax.axis_size(("z", "xl", "c"))
    members = lax.axis_size(RING)
    head, tail = deal(orbitals)
    head = exchange(head, "xh")
    below_head = passed_along(head, 1)
    tail = exchange(tail, "xh")
    below_tail = passed_along(tail, 1)
    above_head = passed_along(head, -1)
    above_tail = passed_along(tail, -1)

    def tiles(order, *operands):
        units = call(functools.partial(tiles_kernel, order), (UNITS, ROWS, UNIT), *operands)
        pair = exchange(units.reshape(2, UNITS // 2, ROWS, UNIT), "c")
        return (pair[0] + pair[1]).reshape(members, -1, ROWS, UNIT)

    inner = tiles(INNER, head, tail)
    below_head, below_tail, inner = lax.optimization_barrier((below_head, below_tail, inner))
    outer = tiles(OUTER, head, tail, below_head, below_tail)
    share = exchange(jnp.concatenate([inner, outer], 1), RING)
    share = share.sum(0) / points
    both = spread(share, RING)
    following = passed_along(both[:, 2:], -1)
    shape = (GROUPS, bands, orbitals.shape[1] // GROUPS)
    part = call(apply_kernel, shape, head, tail, below_head, below_tail, spread(both, "c"))
    part, following = lax.optimization_barrier((part, following))
    partner = lax.ppermute(following, "c", [(0, 1), (1, 0)])
    corrected = pl.pallas_call(
        above_kernel,
        out_shape=jax.ShapeDtypeStruct(shape, jnp.float32),
        in_specs=[pl.BlockSpec(memory_space=pltpu.SMEM)] + [pl.BlockSpec(memory_space=pltpu.VMEM)] * 5,
        compiler_params=pltpu.CompilerParams(vmem_limit_bytes=16 << 20),
    )(lax.axis_index("c").reshape(1), part, above_head, above_tail, following, partner)
    return collect(exchange(corrected, "xh"))


def solution(mesh):
    fine = Mesh(mesh.devices.reshape(8, 4, 8, 2, 2), ("y", "xh", "z", "xl", "c"))
    spec = P(("y", "xh"), ("z", "xl", "c"))
    return jax.shard_map(shards, mesh=fine, in_specs=(spec,), out_specs=spec, check_vma=False)
```

```python
import functools

import jax
import jax.numpy as jnp
from jax import lax
from jax.experimental import pallas as pl
from jax.experimental.pallas import tpu as pltpu
from jax.sharding import Mesh, PartitionSpec as P


RING = ("xh", "z", "xl")
ROWS, UNIT = 8, 128
GROUPS = 4
UNITS = 256
NT = ((1,), (1,))
NN = ((1,), (0,))
TN = ((0,), (0,))


def passed_along(block, distance):
    count = lax.axis_size("y")
    return lax.ppermute(block, "y", [(i, (i + distance) % count) for i in range(count)])


def exchange(pieces, axes):
    return lax.all_to_all(pieces, axes, 0, 0)


def spread(piece, axes):
    count = lax.axis_size(axes)
    return exchange(jnp.broadcast_to(piece[None], (count, *piece.shape)), axes)


def halves(value):
    high = value.astype(jnp.bfloat16)
    return high, (value - high.astype(jnp.float32)).astype(jnp.bfloat16)


def product(left, right, dims):
    dot = functools.partial(
        lax.dot_general, dimension_numbers=(dims, ((), ())), preferred_element_type=jnp.float32
    )
    return dot(left[0], right[0]) + (dot(left[0], right[1]) + dot(left[1], right[0]))


def cut(pair, rows=slice(None), columns=slice(None)):
    return tuple(value[rows, columns] for value in pair)


def call(kernel, outs, *operands):
    return pl.pallas_call(
        kernel,
        out_shape=jax.ShapeDtypeStruct(outs, jnp.float32),
        compiler_params=pltpu.CompilerParams(vmem_limit_bytes=16 << 20),
    )(*operands)


def moved(copies, sems):
    copies = [pltpu.make_async_copy(*copy, sems.at[i]) for i, copy in enumerate(copies)]
    for copy in copies:
        copy.start()
    for copy in copies:
        copy.wait()


def deal_kernel(block, head, tail, sems):
    split, width = head.shape[2], head.shape[2] + tail.shape[2]
    copies = [(block.at[:, width * a : width * a + split], head.at[a]) for a in range(GROUPS)]
    copies += [(block.at[:, width * a + split : width * (a + 1)], tail.at[a]) for a in range(GROUPS)]
    moved(copies, sems)


def deal(block):
    bands, width = block.shape[0], block.shape[1] // GROUPS
    split = width // 3 * 2
    return pl.pallas_call(
        deal_kernel,
        out_shape=[
            jax.ShapeDtypeStruct((GROUPS, bands, size), jnp.float32) for size in (split, width - split)
        ],
        in_specs=[pl.BlockSpec(memory_space=pltpu.HBM)],
        out_specs=[pl.BlockSpec(memory_space=pltpu.VMEM)] * 2,
        scratch_shapes=[pltpu.SemaphoreType.DMA((2 * GROUPS,))],
        compiler_params=pltpu.CompilerParams(vmem_limit_bytes=4 << 20),
    )(block)


def collect_kernel(head, tail, block, sems):
    split, width = head.shape[2], head.shape[2] + tail.shape[2]
    copies = [(head.at[a], block.at[:, width * a : width * a + split]) for a in range(GROUPS)]
    copies += [(tail.at[a], block.at[:, width * a + split : width * (a + 1)]) for a in range(GROUPS)]
    moved(copies, sems)


def collect(head, tail):
    return pl.pallas_call(
        collect_kernel,
        out_shape=jax.ShapeDtypeStruct((head.shape[1], GROUPS * (head.shape[2] + tail.shape[2])), jnp.float32),
        in_specs=[pl.BlockSpec(memory_space=pltpu.VMEM)] * 2,
        out_specs=pl.BlockSpec(memory_space=pltpu.HBM),
        scratch_shapes=[pltpu.SemaphoreType.DMA((2 * GROUPS,))],
        compiler_params=pltpu.CompilerParams(vmem_limit_bytes=4 << 20),
    )(head, tail)


def joined(head_ref, tail_ref):
    value = jnp.concatenate([head_ref[...], tail_ref[...]], -1)
    return value.reshape(-1, value.shape[-1])


def tiles_kernel(order, row_head, row_tail, *refs):
    *other_refs, units_ref = refs
    bands = row_head.shape[1]
    rows = halves(joined(row_head, row_tail))
    other = halves(joined(*other_refs)) if other_refs else rows

    def put(index, value):
        count = value.shape[0] // ROWS
        units_ref[20 * index : 20 * index + count] = value.reshape(count, ROWS, UNIT)

    strips = []
    for a, first, last in order:
        left = cut(rows, slice(bands * a, bands * (a + 1)))
        strips.append(product(left, cut(other, slice(bands * first, bands * last)), NT))
    wide, middle, narrow, single = strips
    columns = [wide[:, UNIT * i : UNIT * (i + 1)] for i in range(5)]
    columns += [middle[:, UNIT * i : UNIT * (i + 1)] for i in range(3)]
    columns += [narrow[:, UNIT * i : UNIT * (i + 1)] for i in range(2)]
    columns += [single[:, :UNIT], jnp.concatenate([middle[:, 384:], single[:, UNIT:]], 1)]
    columns += [jnp.concatenate([narrow[: bands // 2, 256:], narrow[bands // 2 :, 256:]], 1)]
    for index, value in enumerate(columns):
        put(index, value)
    units_ref[250:] = jnp.zeros((6, ROWS, UNIT), jnp.float32)


def strips_of(units_of):
    half = UNITS // 2

    def get(index, count=20):
        start, stop = 20 * index, 20 * index + count
        parts = []
        for core in range(2):
            low, high = max(start, half * core) - half * core, min(stop, half * (core + 1)) - half * core
            if low < high:
                part = units_of(core, slice(low // 2, high // 2))
                parts.append(part.reshape(high - low, ROWS, UNIT))
        value = parts[0] if len(parts) == 1 else jnp.concatenate(parts)
        return value.reshape(count * ROWS, UNIT)

    mixed, tail = get(11), get(12, 10)
    wide = jnp.concatenate([get(i) for i in range(5)], 1)
    middle = jnp.concatenate([get(5), get(6), get(7), mixed[:, :96]], 1)
    narrow = jnp.concatenate([get(8), get(9), jnp.concatenate([tail[:, :64], tail[:, 64:]])], 1)
    single = jnp.concatenate([get(10), mixed[:, 96:]], 1)
    return wide, middle, narrow, single


def apply_kernel(row_head, row_tail, below_head, below_tail, units_ref, out_ref):
    bands = row_head.shape[1]
    row = joined(row_head, row_tail)
    rows = halves(row)
    below = halves(joined(below_head, below_tail))
    inner = strips_of(lambda core, pairs: units_ref[core, pairs, 0:2])[::-1]
    outer = strips_of(lambda core, pairs: units_ref[core, pairs, 2:4])
    fix = []
    for a in range(GROUPS):
        width = bands * (a + 1)
        shift = lax.broadcasted_iota(jnp.int32, (bands, width), 1) - lax.broadcasted_iota(
            jnp.int32, (bands, width), 0
        )
        own = halves(jnp.where(shift == bands * a, inner[a] - 1.0, inner[a]))
        total = product(own, cut(rows, slice(0, width)), NN)
        total += product(halves(outer[a]), cut(below, slice(bands * a, None)), NN)
        fix.append(total)
        if a > 0:
            back = product(
                cut(own, slice(None), slice(0, bands * a)), cut(rows, slice(bands * a, width)), TN
            )
            for b in range(a):
                fix[b] += back[bands * b : bands * (b + 1)]
    for a in range(GROUPS):
        out_ref[a] = row[bands * a : bands * (a + 1)] - 0.5 * fix[a]


def above_kernel(core_ref, part_ref, above_head, above_tail, own_ref, partner_ref, head_out, tail_out):
    first = core_ref[0] == 0
    split = head_out.shape[2]
    bands = part_ref.shape[1]
    above = halves(joined(above_head, above_tail))

    def units_of(core, pairs):
        own, partner = own_ref[pairs], partner_ref[pairs]
        return jnp.where(first, own, partner) if core == 0 else jnp.where(first, partner, own)

    strips = strips_of(units_of)
    fix = [None] * GROUPS
    for b in range(GROUPS):
        back = product(halves(strips[b]), cut(above, slice(bands * b, bands * (b + 1))), TN)
        for a in range(b, GROUPS):
            term = back[bands * (a - b) : bands * (a - b + 1)]
            fix[a] = term if b == 0 else fix[a] + term
    for a in range(GROUPS):
        corrected = part_ref[a] - 0.5 * fix[a]
        head_out[a] = corrected[:, :split]
        tail_out[a] = corrected[:, split:]


INNER = [(3, 0, 4), (2, 0, 3), (1, 0, 2), (0, 0, 1)]
OUTER = [(0, 0, 4), (1, 1, 4), (2, 2, 4), (3, 3, 4)]


def shards(orbitals):
    bands = orbitals.shape[0]
    points = orbitals.shape[1] * lax.axis_size(("z", "xl", "c"))
    members = lax.axis_size(RING)
    head, tail = deal(pltpu.with_memory_space_constraint(orbitals, pltpu.HBM))
    head = exchange(head, "xh")
    below_head = passed_along(head, 1)
    tail = exchange(tail, "xh")
    below_tail = passed_along(tail, 1)
    above_head = passed_along(head, -1)
    above_tail = passed_along(tail, -1)

    def tiles(order, *operands):
        units = call(functools.partial(tiles_kernel, order), (UNITS, ROWS, UNIT), *operands)
        pair = exchange(units.reshape(2, UNITS // 2, ROWS, UNIT), "c")
        return (pair[0] + pair[1]).reshape(members, -1, ROWS, UNIT)

    inner = tiles(INNER, head, tail)
    below_head, below_tail, inner = lax.optimization_barrier((below_head, below_tail, inner))
    outer = tiles(OUTER, head, tail, below_head, below_tail)
    share = exchange(jnp.concatenate([inner, outer], 1), RING)
    share = share.sum(0) / points
    both = spread(share, RING)
    following = passed_along(both[:, 2:], -1)
    shape = (GROUPS, bands, orbitals.shape[1] // GROUPS)
    part = call(apply_kernel, shape, head, tail, below_head, below_tail, spread(both, "c"))
    part, following = lax.optimization_barrier((part, following))
    partner = lax.ppermute(following, "c", [(0, 1), (1, 0)])
    head, tail = pl.pallas_call(
        above_kernel,
        out_shape=[jax.ShapeDtypeStruct(chunk.shape, jnp.float32) for chunk in (head, tail)],
        in_specs=[pl.BlockSpec(memory_space=pltpu.SMEM)] + [pl.BlockSpec(memory_space=pltpu.VMEM)] * 5,
        compiler_params=pltpu.CompilerParams(vmem_limit_bytes=16 << 20),
    )(lax.axis_index("c").reshape(1), part, above_head, above_tail, following, partner)
    return collect(exchange(head, "xh"), exchange(tail, "xh"))


def solution(mesh):
    fine = Mesh(mesh.devices.reshape(8, 4, 8, 2, 2), ("y", "xh", "z", "xl", "c"))
    spec = P(("y", "xh"), ("z", "xl", "c"))
    return jax.shard_map(shards, mesh=fine, in_specs=(spec,), out_specs=spec, check_vma=False)
```

```python
import functools

import jax
import jax.numpy as jnp
from jax import lax
from jax.experimental import pallas as pl
from jax.experimental.pallas import tpu as pltpu
from jax.sharding import Mesh, PartitionSpec as P


RING = ("xh", "z", "xl")
ROWS, UNIT = 8, 128
GROUPS = 4
UNITS = 256
NT = ((1,), (1,))
NN = ((1,), (0,))
TN = ((0,), (0,))


def passed_along(block, distance):
    count = lax.axis_size("y")
    return lax.ppermute(block, "y", [(i, (i + distance) % count) for i in range(count)])


def exchange(pieces, axes):
    return lax.all_to_all(pieces, axes, 0, 0)


def spread(piece, axes):
    count = lax.axis_size(axes)
    return exchange(jnp.broadcast_to(piece[None], (count, *piece.shape)), axes)


def halves(value):
    high = value.astype(jnp.bfloat16)
    return high, (value - high.astype(jnp.float32)).astype(jnp.bfloat16)


def product(left, right, dims):
    dot = functools.partial(
        lax.dot_general, dimension_numbers=(dims, ((), ())), preferred_element_type=jnp.float32
    )
    return dot(left[0], right[0]) + (dot(left[0], right[1]) + dot(left[1], right[0]))


def cut(pair, rows=slice(None), columns=slice(None)):
    return tuple(value[rows, columns] for value in pair)


def call(kernel, outs, *operands):
    return pl.pallas_call(
        kernel,
        out_shape=jax.ShapeDtypeStruct(outs, jnp.float32),
        compiler_params=pltpu.CompilerParams(vmem_limit_bytes=16 << 20),
    )(*operands)


def moved(copies, sems):
    copies = [pltpu.make_async_copy(*copy, sems.at[i]) for i, copy in enumerate(copies)]
    for copy in copies:
        copy.start()
    for copy in copies:
        copy.wait()


def deal_kernel(block, head, tail, sems):
    split, width = head.shape[2], head.shape[2] + tail.shape[2]
    copies = [(block.at[:, width * a : width * a + split], head.at[a]) for a in range(GROUPS)]
    copies += [(block.at[:, width * a + split : width * (a + 1)], tail.at[a]) for a in range(GROUPS)]
    moved(copies, sems)


def deal(block):
    bands, width = block.shape[0], block.shape[1] // GROUPS
    split = width // 3 * 2
    return pl.pallas_call(
        deal_kernel,
        out_shape=[
            jax.ShapeDtypeStruct((GROUPS, bands, size), jnp.float32) for size in (split, width - split)
        ],
        in_specs=[pl.BlockSpec(memory_space=pltpu.HBM)],
        out_specs=[pl.BlockSpec(memory_space=pltpu.VMEM)] * 2,
        scratch_shapes=[pltpu.SemaphoreType.DMA((2 * GROUPS,))],
        compiler_params=pltpu.CompilerParams(vmem_limit_bytes=4 << 20),
    )(block)


def collect_kernel(quarters, block, sems):
    width = quarters.shape[2]
    moved([(quarters.at[a], block.at[:, width * a : width * (a + 1)]) for a in range(GROUPS)], sems)


def collect(quarters):
    return pl.pallas_call(
        collect_kernel,
        out_shape=jax.ShapeDtypeStruct((quarters.shape[1], GROUPS * quarters.shape[2]), jnp.float32),
        in_specs=[pl.BlockSpec(memory_space=pltpu.VMEM)],
        out_specs=pl.BlockSpec(memory_space=pltpu.HBM),
        scratch_shapes=[pltpu.SemaphoreType.DMA((GROUPS,))],
        compiler_params=pltpu.CompilerParams(vmem_limit_bytes=4 << 20),
    )(quarters)


def joined(head_ref, tail_ref):
    value = jnp.concatenate([head_ref[...], tail_ref[...]], -1)
    return value.reshape(-1, value.shape[-1])


def tiles_kernel(order, row_head, row_tail, *refs):
    *other_refs, units_ref = refs
    bands = row_head.shape[1]
    rows = halves(joined(row_head, row_tail))
    other = halves(joined(*other_refs)) if other_refs else rows

    def put(index, value):
        count = value.shape[0] // ROWS
        units_ref[20 * index : 20 * index + count] = value.reshape(count, ROWS, UNIT)

    strips = []
    for a, first, last in order:
        left = cut(rows, slice(bands * a, bands * (a + 1)))
        strips.append(product(left, cut(other, slice(bands * first, bands * last)), NT))
    wide, middle, narrow, single = strips
    columns = [wide[:, UNIT * i : UNIT * (i + 1)] for i in range(5)]
    columns += [middle[:, UNIT * i : UNIT * (i + 1)] for i in range(3)]
    columns += [narrow[:, UNIT * i : UNIT * (i + 1)] for i in range(2)]
    columns += [single[:, :UNIT], jnp.concatenate([middle[:, 384:], single[:, UNIT:]], 1)]
    columns += [jnp.concatenate([narrow[: bands // 2, 256:], narrow[bands // 2 :, 256:]], 1)]
    for index, value in enumerate(columns):
        put(index, value)
    units_ref[250:] = jnp.zeros((6, ROWS, UNIT), jnp.float32)


def strips_of(units_of):
    half = UNITS // 2

    def get(index, count=20):
        start, stop = 20 * index, 20 * index + count
        parts = []
        for core in range(2):
            low, high = max(start, half * core) - half * core, min(stop, half * (core + 1)) - half * core
            if low < high:
                part = units_of(core, slice(low // 2, high // 2))
                parts.append(part.reshape(high - low, ROWS, UNIT))
        value = parts[0] if len(parts) == 1 else jnp.concatenate(parts)
        return value.reshape(count * ROWS, UNIT)

    mixed, tail = get(11), get(12, 10)
    wide = jnp.concatenate([get(i) for i in range(5)], 1)
    middle = jnp.concatenate([get(5), get(6), get(7), mixed[:, :96]], 1)
    narrow = jnp.concatenate([get(8), get(9), jnp.concatenate([tail[:, :64], tail[:, 64:]])], 1)
    single = jnp.concatenate([get(10), mixed[:, 96:]], 1)
    return wide, middle, narrow, single


def apply_kernel(row_head, row_tail, below_head, below_tail, units_ref, out_ref):
    bands = row_head.shape[1]
    row = joined(row_head, row_tail)
    rows = halves(row)
    below = halves(joined(below_head, below_tail))
    inner = strips_of(lambda core, pairs: units_ref[core, pairs, 0:2])[::-1]
    outer = strips_of(lambda core, pairs: units_ref[core, pairs, 2:4])
    fix = []
    for a in range(GROUPS):
        width = bands * (a + 1)
        shift = lax.broadcasted_iota(jnp.int32, (bands, width), 1) - lax.broadcasted_iota(
            jnp.int32, (bands, width), 0
        )
        own = halves(jnp.where(shift == bands * a, inner[a] - 1.0, inner[a]))
        total = product(own, cut(rows, slice(0, width)), NN)
        total += product(halves(outer[a]), cut(below, slice(bands * a, None)), NN)
        fix.append(total)
        if a > 0:
            back = product(
                cut(own, slice(None), slice(0, bands * a)), cut(rows, slice(bands * a, width)), TN
            )
            for b in range(a):
                fix[b] += back[bands * b : bands * (b + 1)]
    for a in range(GROUPS):
        out_ref[a] = row[bands * a : bands * (a + 1)] - 0.5 * fix[a]


def above_kernel(part_ref, above_head, above_tail, own_ref, partner_ref, out_ref):
    first = lax.axis_index("c") == 0
    bands = part_ref.shape[1]
    above = halves(joined(above_head, above_tail))

    def units_of(core, pairs):
        own, partner = own_ref[pairs], partner_ref[pairs]
        return jnp.where(first, own, partner) if core == 0 else jnp.where(first, partner, own)

    strips = strips_of(units_of)
    fix = [None] * GROUPS
    for b in range(GROUPS):
        back = product(halves(strips[b]), cut(above, slice(bands * b, bands * (b + 1))), TN)
        for a in range(b, GROUPS):
            term = back[bands * (a - b) : bands * (a - b + 1)]
            fix[a] = term if b == 0 else fix[a] + term
    for a in range(GROUPS):
        out_ref[a] = part_ref[a] - 0.5 * fix[a]


INNER = [(3, 0, 4), (2, 0, 3), (1, 0, 2), (0, 0, 1)]
OUTER = [(0, 0, 4), (1, 1, 4), (2, 2, 4), (3, 3, 4)]


def shards(orbitals):
    bands = orbitals.shape[0]
    points = orbitals.shape[1] * lax.axis_size(("z", "xl", "c"))
    members = lax.axis_size(RING)
    head, tail = deal(pltpu.with_memory_space_constraint(orbitals, pltpu.HBM))
    head = exchange(head, "xh")
    below_head = passed_along(head, 1)
    tail = exchange(tail, "xh")
    below_tail = passed_along(tail, 1)
    above_head = passed_along(head, -1)
    above_tail = passed_along(tail, -1)

    def tiles(order, *operands):
        units = call(functools.partial(tiles_kernel, order), (UNITS, ROWS, UNIT), *operands)
        pair = exchange(units.reshape(2, UNITS // 2, ROWS, UNIT), "c")
        return (pair[0] + pair[1]).reshape(members, -1, ROWS, UNIT)

    inner = tiles(INNER, head, tail)
    below_head, below_tail, inner = lax.optimization_barrier((below_head, below_tail, inner))
    outer = tiles(OUTER, head, tail, below_head, below_tail)
    share = exchange(jnp.concatenate([inner, outer], 1), RING)
    share = share.sum(0) / points
    both = spread(share, RING)
    following = passed_along(both[:, 2:], -1)
    shape = (GROUPS, bands, orbitals.shape[1] // GROUPS)
    part = call(apply_kernel, shape, head, tail, below_head, below_tail, spread(both, "c"))
    part, following = lax.optimization_barrier((part, following))
    partner = lax.ppermute(following, "c", [(0, 1), (1, 0)])
    corrected = pl.pallas_call(
        above_kernel,
        out_shape=jax.ShapeDtypeStruct(shape, jnp.float32),
        compiler_params=pltpu.CompilerParams(vmem_limit_bytes=16 << 20),
    )(part, above_head, above_tail, following, partner)
    return collect(exchange(corrected, "xh"))


def solution(mesh):
    fine = Mesh(mesh.devices.reshape(8, 4, 8, 2, 2), ("y", "xh", "z", "xl", "c"))
    spec = P(("y", "xh"), ("z", "xl", "c"))
    return jax.shard_map(shards, mesh=fine, in_specs=(spec,), out_specs=spec, check_vma=False)
```

```python
import functools

import jax
import jax.numpy as jnp
from jax import lax
from jax.experimental import pallas as pl
from jax.experimental.pallas import tpu as pltpu
from jax.sharding import Mesh, PartitionSpec as P


RING = ("xh", "z", "xl")
ROWS, UNIT = 8, 128
GROUPS = 4
UNITS = 256
NT = ((1,), (1,))
NN = ((1,), (0,))
TN = ((0,), (0,))


def passed_along(block, distance):
    count = lax.axis_size("y")
    return lax.ppermute(block, "y", [(i, (i + distance) % count) for i in range(count)])


def exchange(pieces, axes):
    return lax.all_to_all(pieces, axes, 0, 0)


def spread(piece, axes):
    count = lax.axis_size(axes)
    return exchange(jnp.broadcast_to(piece[None], (count, *piece.shape)), axes)


def halves(value):
    high = value.astype(jnp.bfloat16)
    return high, (value - high.astype(jnp.float32)).astype(jnp.bfloat16)


def product(left, right, dims):
    dot = functools.partial(
        lax.dot_general, dimension_numbers=(dims, ((), ())), preferred_element_type=jnp.float32
    )
    return dot(left[0], right[0]) + (dot(left[0], right[1]) + dot(left[1], right[0]))


def cut(pair, rows=slice(None), columns=slice(None)):
    return tuple(value[rows, columns] for value in pair)


def call(kernel, outs, *operands):
    return pl.pallas_call(
        kernel,
        out_shape=jax.ShapeDtypeStruct(outs, jnp.float32),
        compiler_params=pltpu.CompilerParams(vmem_limit_bytes=16 << 20),
    )(*operands)


def moved(copies, sems):
    copies = [pltpu.make_async_copy(*copy, sems.at[i]) for i, copy in enumerate(copies)]
    for copy in copies:
        copy.start()
    for copy in copies:
        copy.wait()


def deal_kernel(block, head, tail, sems):
    split, width = head.shape[2], head.shape[2] + tail.shape[2]
    copies = [(block.at[:, width * a : width * a + split], head.at[a]) for a in range(GROUPS)]
    copies += [(block.at[:, width * a + split : width * (a + 1)], tail.at[a]) for a in range(GROUPS)]
    moved(copies, sems)


def deal(block):
    bands, width = block.shape[0], block.shape[1] // GROUPS
    split = width // 3 * 2
    return pl.pallas_call(
        deal_kernel,
        out_shape=[
            jax.ShapeDtypeStruct((GROUPS, bands, size), jnp.float32) for size in (split, width - split)
        ],
        in_specs=[pl.BlockSpec(memory_space=pltpu.HBM)],
        out_specs=[pl.BlockSpec(memory_space=pltpu.VMEM)] * 2,
        scratch_shapes=[pltpu.SemaphoreType.DMA((2 * GROUPS,))],
        compiler_params=pltpu.CompilerParams(vmem_limit_bytes=4 << 20),
    )(block)


def collect_kernel(quarters, block, sems):
    width = quarters.shape[2]
    moved([(quarters.at[a], block.at[:, width * a : width * (a + 1)]) for a in range(GROUPS)], sems)


def collect(quarters):
    return pl.pallas_call(
        collect_kernel,
        out_shape=jax.ShapeDtypeStruct((quarters.shape[1], GROUPS * quarters.shape[2]), jnp.float32),
        in_specs=[pl.BlockSpec(memory_space=pltpu.VMEM)],
        out_specs=pl.BlockSpec(memory_space=pltpu.HBM),
        scratch_shapes=[pltpu.SemaphoreType.DMA((GROUPS,))],
        compiler_params=pltpu.CompilerParams(vmem_limit_bytes=4 << 20),
    )(quarters)


def joined(head_ref, tail_ref):
    value = jnp.concatenate([head_ref[...], tail_ref[...]], -1)
    return value.reshape(-1, value.shape[-1])


def tiles_kernel(order, row_head, row_tail, *refs):
    *other_refs, units_ref = refs
    bands = row_head.shape[1]
    rows = halves(joined(row_head, row_tail))
    other = halves(joined(*other_refs)) if other_refs else rows

    def put(index, value):
        count = value.shape[0] // ROWS
        units_ref[20 * index : 20 * index + count] = value.reshape(count, ROWS, UNIT)

    strips = []
    for a, first, last in order:
        left = cut(rows, slice(bands * a, bands * (a + 1)))
        strips.append(product(left, cut(other, slice(bands * first, bands * last)), NT))
    wide, middle, narrow, single = strips
    columns = [wide[:, UNIT * i : UNIT * (i + 1)] for i in range(5)]
    columns += [middle[:, UNIT * i : UNIT * (i + 1)] for i in range(3)]
    columns += [narrow[:, UNIT * i : UNIT * (i + 1)] for i in range(2)]
    columns += [single[:, :UNIT], jnp.concatenate([middle[:, 384:], single[:, UNIT:]], 1)]
    columns += [jnp.concatenate([narrow[: bands // 2, 256:], narrow[bands // 2 :, 256:]], 1)]
    for index, value in enumerate(columns):
        put(index, value)
    units_ref[250:] = jnp.zeros((6, ROWS, UNIT), jnp.float32)


def strips_of(units_of):
    half = UNITS // 2

    def get(index, count=20):
        start, stop = 20 * index, 20 * index + count
        parts = []
        for core in range(2):
            low, high = max(start, half * core) - half * core, min(stop, half * (core + 1)) - half * core
            if low < high:
                part = units_of(core, slice(low // 2, high // 2))
                parts.append(part.reshape(high - low, ROWS, UNIT))
        value = parts[0] if len(parts) == 1 else jnp.concatenate(parts)
        return value.reshape(count * ROWS, UNIT)

    mixed, tail = get(11), get(12, 10)
    wide = jnp.concatenate([get(i) for i in range(5)], 1)
    middle = jnp.concatenate([get(5), get(6), get(7), mixed[:, :96]], 1)
    narrow = jnp.concatenate([get(8), get(9), jnp.concatenate([tail[:, :64], tail[:, 64:]])], 1)
    single = jnp.concatenate([get(10), mixed[:, 96:]], 1)
    return wide, middle, narrow, single


def apply_kernel(row_head, row_tail, below_head, below_tail, units_ref, out_ref):
    bands = row_head.shape[1]
    row = joined(row_head, row_tail)
    rows = halves(row)
    below = halves(joined(below_head, below_tail))
    inner = strips_of(lambda core, pairs: units_ref[core, pairs, 0:2])[::-1]
    outer = strips_of(lambda core, pairs: units_ref[core, pairs, 2:4])
    fix = []
    for a in range(GROUPS):
        width = bands * (a + 1)
        shift = lax.broadcasted_iota(jnp.int32, (bands, width), 1) - lax.broadcasted_iota(
            jnp.int32, (bands, width), 0
        )
        own = halves(jnp.where(shift == bands * a, inner[a] - 1.0, inner[a]))
        total = product(own, cut(rows, slice(0, width)), NN)
        total += product(halves(outer[a]), cut(below, slice(bands * a, None)), NN)
        fix.append(total)
        if a > 0:
            back = product(
                cut(own, slice(None), slice(0, bands * a)), cut(rows, slice(bands * a, width)), TN
            )
            for b in range(a):
                fix[b] += back[bands * b : bands * (b + 1)]
    for a in range(GROUPS):
        out_ref[a] = row[bands * a : bands * (a + 1)] - 0.5 * fix[a]


def above_kernel(part_ref, above_head, above_tail, own_ref, partner_ref, out_ref):
    first = lax.axis_index("c") == 0
    bands = part_ref.shape[1]
    above = halves(joined(above_head, above_tail))

    def units_of(core, pairs):
        own, partner = own_ref[pairs], partner_ref[pairs]
        return jnp.where(first, own, partner) if core == 0 else jnp.where(first, partner, own)

    strips = strips_of(units_of)
    fix = [None] * GROUPS
    for b in range(GROUPS):
        back = product(halves(strips[b]), cut(above, slice(bands * b, bands * (b + 1))), TN)
        for a in range(b, GROUPS):
            term = back[bands * (a - b) : bands * (a - b + 1)]
            fix[a] = term if b == 0 else fix[a] + term
    for a in range(GROUPS):
        out_ref[a] = part_ref[a] - 0.5 * fix[a]


def sums_kernel(inner_ref, outer_ref, out_ref):
    out_ref[:, :2] = inner_ref[0] + inner_ref[1]
    out_ref[:, 2:] = outer_ref[0] + outer_ref[1]


def share_kernel(points, parts_ref, out_ref):
    out_ref[...] = jnp.broadcast_to((parts_ref[...].sum(0) / points)[None], out_ref.shape)


INNER = [(3, 0, 4), (2, 0, 3), (1, 0, 2), (0, 0, 1)]
OUTER = [(0, 0, 4), (1, 1, 4), (2, 2, 4), (3, 3, 4)]


def shards(orbitals):
    bands = orbitals.shape[0]
    points = orbitals.shape[1] * lax.axis_size(("z", "xl", "c"))
    members = lax.axis_size(RING)
    head, tail = deal(pltpu.with_memory_space_constraint(orbitals, pltpu.HBM))
    head = exchange(head, "xh")
    below_head = passed_along(head, 1)
    tail = exchange(tail, "xh")
    below_tail = passed_along(tail, 1)
    above_head = passed_along(head, -1)
    above_tail = passed_along(tail, -1)

    def tiles(order, *operands):
        units = call(functools.partial(tiles_kernel, order), (UNITS, ROWS, UNIT), *operands)
        pair = exchange(units.reshape(2, UNITS // 2, ROWS, UNIT), "c")
        return pair.reshape(2, members, -1, ROWS, UNIT)

    inner = tiles(INNER, head, tail)
    below_head, below_tail, inner = lax.optimization_barrier((below_head, below_tail, inner))
    outer = tiles(OUTER, head, tail, below_head, below_tail)
    parts = exchange(call(sums_kernel, (members, 4, ROWS, UNIT), inner, outer), RING)
    shares = call(functools.partial(share_kernel, points), parts.shape, parts)
    both = exchange(shares, RING)
    following = passed_along(both[:, 2:], -1)
    shape = (GROUPS, bands, orbitals.shape[1] // GROUPS)
    part = call(apply_kernel, shape, head, tail, below_head, below_tail, spread(both, "c"))
    part, following = lax.optimization_barrier((part, following))
    partner = lax.ppermute(following, "c", [(0, 1), (1, 0)])
    corrected = pl.pallas_call(
        above_kernel,
        out_shape=jax.ShapeDtypeStruct(shape, jnp.float32),
        compiler_params=pltpu.CompilerParams(vmem_limit_bytes=16 << 20),
    )(part, above_head, above_tail, following, partner)
    return collect(exchange(corrected, "xh"))


def solution(mesh):
    fine = Mesh(mesh.devices.reshape(8, 4, 8, 2, 2), ("y", "xh", "z", "xl", "c"))
    spec = P(("y", "xh"), ("z", "xl", "c"))
    return jax.shard_map(shards, mesh=fine, in_specs=(spec,), out_specs=spec, check_vma=False)
```
